32 devices in a mesh: beam: 2 (over x), wide: 16 (over z, y, core).
Axes of the slice: x: 2, y: 2, z: 4, core: 2. Of those that a mesh axis runs over, the one named last changes fastest.
Arguments:
- filterbank: bfloat16 [2, 4096, 4096], P('beam', 'wide'), parts along dimension 0, may hold values from -100 to 100
- channel_mask: int32 [8192], P(('beam', 'wide')), parts along dimension 0, may hold values 0 or 1
- band_edges: int32 [7], replicated, may hold values from 385 to 3711, as said below
- dm_delays: int32 [16], replicated, may hold values from 0 to 2047
Outputs:
- series: float32 [2, 16, 4096], P('beam', 'wide'), parts along dimension 0
The draws below stay inside these ranges and needn't reach their ends.
There are 2 independent parts, one for each index of `beam`. The reference program is written for one: setup_inputs(seed, part) draws one part's arguments, and reference() takes and returns one part's arrays. A program takes and returns all parts, laid end to end along the dimension named above; an argument that names none is the same for every part. Nothing has to cross between parts.
Inputs may be any that keep to these rules, and one draw needn't show every extreme that they name: `band_edges`: strictly increasing; entry i lies at (i + 1) * 512 up to a shift of less than 128.
All inputs are finite; a program needn't handle non-finite values. No bound on the sum of `channel_mask` on one device may be relied on, other than what follows from the above.
Results may differ from the reference program's by a relative error of at most 0.0063.
Values may be sent and summed in bfloat16 or wider, within the bound.
A program may use at most 64 MiB of HBM per device.

```python
import math
import jax
import jax.numpy as jnp
from jax import lax

C = 4096
NT = 4096
NBLK = 8
NB = 1
NDM = 16
NBAND = 8


def draw_filterbank(key, part):
    key_noise, key_gain, key_time, key_ripple = jax.random.split(key, 4)
    channel_pos = jnp.arange(C, dtype=jnp.float32)
    ramp = 1.0 + 2.0 * channel_pos / (C - 1)
    offset = jax.random.uniform(key_ripple, (), minval=0.0, maxval=2.0 * math.pi)
    ripple = jnp.exp(jnp.sin(2.0 * math.pi * channel_pos * NBAND / (3.0 * C) + offset))
    noise = jax.random.normal(key_noise, (NB, C, NT))
    gain = jnp.exp(jax.random.uniform(key_gain, (C,)) * math.log(10.0))
    time_scale = jnp.exp(jax.random.uniform(key_time, (NB, 1, NT)) * math.log(10.0))
    values = noise * (ramp * ripple * gain)[None, :, None] * time_scale / 20.0
    return jnp.clip(values, -100.0, 100.0).astype(jnp.bfloat16)


def draw_band_edges(key, part):
    spacing = C // NBAND
    jitter = C // (4 * NBAND)
    offsets = jax.random.randint(key, (NBAND - 1,), -(jitter - 1), jitter)
    offsets = offsets.at[0].set(-(jitter - 1)).at[NBAND - 2].set(jitter - 1)
    return (jnp.arange(1, NBAND, dtype=jnp.int32) * spacing + offsets).astype(jnp.int32)


def plant(values, key, least, top_value):
    longest = values.shape.index(max(values.shape))
    spots = []
    for shift in (0, 1):
        where = [jax.random.randint(jax.random.fold_in(key, axis), (), 0, length) for axis, length in enumerate(values.shape)]
        where[longest] = (where[longest] + shift) % values.shape[longest]
        spots.append(tuple(where))
    return values.at[spots[0]].set(least).at[spots[1]].set(top_value)


def setup_inputs(seed: int = 0, part: int = 0) -> dict:
    seeds = jax.random.split(jax.random.key(seed), 5)
    own_keys = jax.random.split(jax.random.fold_in(seeds[4], part), 5)
    return {
        "filterbank": draw_filterbank(jax.random.fold_in(jax.random.fold_in(seeds[4], part), 71), part),
        "channel_mask": plant((jax.random.randint(own_keys[1], (C,), 0, 8) < 7).astype(jnp.int32), jax.random.fold_in(own_keys[1], 1), 0, 1),
        "band_edges": draw_band_edges(jax.random.fold_in(seeds[4], 71), part),
        "dm_delays": plant(jax.random.randint(seeds[3], (NDM,), 0, NT // 2), jax.random.fold_in(seeds[3], 1), 0, (NT // 2) - 1).astype(jnp.int32),
    }


def delay_fractions(first_channel, channel_count, total_channels):
    channel_ids = first_channel + jnp.arange(channel_count, dtype=jnp.int32)
    ratio = 0.5 + 0.5 * (channel_ids.astype(jnp.float32) + 0.5) / total_channels
    return (1.0 / (ratio * ratio) - 1.0) / 3.0

def noise_floors(band_power, band_edges, channels):
    bounds = jnp.concatenate([jnp.zeros((1,), jnp.int32), band_edges.astype(jnp.int32), jnp.full((1,), channels, jnp.int32)])
    widths = (bounds[1:] - bounds[:-1]).astype(jnp.float32)
    return jnp.sqrt(band_power / widths[None, :, None] + 1e-05)

def forward_tables(first_bin, bin_count, samples):
    bin_ids = first_bin + jnp.arange(bin_count, dtype=jnp.int32)
    times = jnp.arange(samples, dtype=jnp.int32)
    product = bin_ids[:, None] * times[None, :] % samples
    angle = product.astype(jnp.float32) * (2.0 * math.pi / samples)
    tables = jnp.stack([jnp.cos(angle), -jnp.sin(angle)], axis=0)
    return tables.reshape(2 * bin_count, samples).astype(jnp.bfloat16)

def inverse_tables(first_bin, bin_count, samples, channels):
    bin_ids = first_bin + jnp.arange(bin_count, dtype=jnp.int32)
    times = jnp.arange(samples, dtype=jnp.int32)
    product = bin_ids[:, None] * times[None, :] % samples
    angle = product.astype(jnp.float32) * (2.0 * math.pi / samples)
    weight = jnp.where(bin_ids == 0, 1.0, 2.0).astype(jnp.float32) / (samples * math.sqrt(channels))
    tables = jnp.stack([weight[:, None] * jnp.cos(angle), -weight[:, None] * jnp.sin(angle)], axis=1)
    return tables.reshape(2 * bin_count, samples).astype(jnp.bfloat16)

def phase_tables(first_bin, bin_count, fractions, dm_delays, samples):
    bin_ids = first_bin + jnp.arange(bin_count, dtype=jnp.int32)
    cycles = (bin_ids[:, None] * dm_delays[None, :]).astype(jnp.float32)
    angle = cycles[:, None, :] * fractions[None, :, None] * (2.0 * math.pi / samples)
    return (jnp.cos(angle).astype(jnp.bfloat16), jnp.sin(angle).astype(jnp.bfloat16))

def dedisperse_block(spec_real, spec_imag, cos_tab, sin_tab):
    spec_real = spec_real.astype(jnp.float32)
    spec_imag = spec_imag.astype(jnp.float32)
    cos_tab = cos_tab.astype(jnp.float32)
    sin_tab = sin_tab.astype(jnp.float32)
    real_part = jnp.einsum('fbc,fcd->fbd', spec_real, cos_tab) - jnp.einsum('fbc,fcd->fbd', spec_imag, sin_tab)
    imag_part = jnp.einsum('fbc,fcd->fbd', spec_real, sin_tab) + jnp.einsum('fbc,fcd->fbd', spec_imag, cos_tab)
    return jnp.stack([real_part, imag_part], axis=1)

def reference(filterbank, channel_mask, band_edges, dm_delays):
    beams, channels, samples = filterbank.shape
    bands = band_edges.shape[0] + 1
    signal = filterbank.astype(jnp.float32).reshape(beams, channels, NBLK, samples // NBLK)
    power = lax.optimization_barrier(jnp.mean(signal * signal, axis=3))
    channel_ids = jnp.arange(channels, dtype=jnp.int32)
    band_ids = lax.optimization_barrier(jnp.sum((band_edges[None, :] <= channel_ids[:, None]).astype(jnp.int32), axis=1))
    member = (band_ids[:, None] == jnp.arange(bands, dtype=jnp.int32)[None, :]).astype(jnp.float32)
    keep = channel_mask.astype(jnp.float32)
    band_power = jnp.einsum('cj,bck->bjk', member * keep[:, None], power, precision=lax.Precision.HIGHEST)
    floors = noise_floors(band_power, band_edges, channels)
    channel_floor = jnp.einsum('cj,bjk->bck', member, floors, precision=lax.Precision.HIGHEST)
    cleaned = (signal / channel_floor[..., None] * keep[None, :, None, None]).reshape(beams, channels, samples).astype(jnp.bfloat16)
    rows_flat = cleaned.reshape(beams * channels, samples)
    rows_turned = rows_flat.T
    bins = samples // 4
    dft_step = math.gcd(bins, 256)

    def spectrum_part(first_bin):
        tables = forward_tables(first_bin, dft_step, samples)
        block = jnp.dot(tables, rows_turned, preferred_element_type=jnp.float32).astype(jnp.bfloat16)
        return block.reshape(2, dft_step, beams, channels)
    firsts = jnp.arange(bins // dft_step, dtype=jnp.int32) * dft_step
    blocks = lax.map(spectrum_part, firsts)
    spectrum = jnp.transpose(blocks, (1, 0, 2, 3, 4)).reshape(2, bins, beams, channels)
    fractions = delay_fractions(0, channels, channels)
    phase_step = math.gcd(bins, 8)

    def dm_part(first_bin):
        spec_part = lax.dynamic_slice_in_dim(spectrum, first_bin, phase_step, 1)
        cos_tab, sin_tab = phase_tables(first_bin, phase_step, fractions, dm_delays, samples)
        return dedisperse_block(spec_part[0], spec_part[1], cos_tab, sin_tab)
    phase_firsts = jnp.arange(bins // phase_step, dtype=jnp.int32) * phase_step
    dm_blocks = lax.map(dm_part, phase_firsts)
    trials = dm_delays.shape[0]
    dm_spectrum = dm_blocks.reshape(bins, 2, beams, trials).astype(jnp.bfloat16)
    flat = dm_spectrum.reshape(bins * 2, beams * trials)
    table = inverse_tables(0, bins, samples, channels)
    series = jnp.dot(flat.T, table, preferred_element_type=jnp.float32)
    return series.reshape(beams, trials, samples)
```

```python
import functools
import math

import jax
import jax.numpy as jnp
import numpy as np
from jax import lax
from jax.experimental import pallas as pl
from jax.experimental.pallas import tpu as pltpu
from jax.sharding import PartitionSpec as P

NBLK = 8
LANES = 128
VMEM = pl.BlockSpec(memory_space=pltpu.VMEM)
SMEM = pl.BlockSpec(memory_space=pltpu.SMEM)
MESH = pl.DeviceIdType.MESH
HIGH = lax.Precision.HIGHEST


def turn_coefficients():
    degree = 5
    nodes = np.cos((np.arange(64) + 0.5) * np.pi / 64) * 0.125 + 0.125
    root = np.sqrt(nodes)
    cos_fit = np.polynomial.Chebyshev.fit(nodes, np.cos(2 * np.pi * root), degree, domain=[0, 0.25])
    sin_fit = np.polynomial.Chebyshev.fit(
        nodes, np.sin(2 * np.pi * root) / root, degree, domain=[0, 0.25]
    )
    as_power = lambda fit: [float(np.float32(v)) for v in fit.convert(kind=np.polynomial.Polynomial).coef]
    return as_power(cos_fit), as_power(sin_fit)


COS_COEF, SIN_COEF = turn_coefficients()


def cos_sin_turns(turns):
    r = turns - jnp.floor(turns + 0.5)
    s = r * r
    c = jnp.full_like(s, COS_COEF[-1])
    q = jnp.full_like(s, SIN_COEF[-1])
    for a, b in zip(COS_COEF[-2::-1], SIN_COEF[-2::-1]):
        c = c * s + a
        q = q * s + b
    return c, q * r


def forward_seeds(samples):
    fine = 32
    quarter = samples // 4
    f = (4 * np.arange(quarter // 4)[None, :] + np.arange(4)[:, None]).reshape(-1)
    coarse = (np.arange(quarter // fine) * fine)[:, None] * f[None, :] % samples
    small = np.arange(fine)[:, None] * f[None, :] % samples
    out = []
    for product in (coarse, small):
        angle = product * (2 * np.pi / samples)
        out += [np.cos(angle), np.sin(angle)]
    return [v.astype(np.float32) for v in out]


def inverse_seeds(samples, channels):
    halves = samples // 16 // LANES
    lane = np.arange(LANES)
    r = np.repeat(np.arange(4), halves)
    h = np.tile(np.arange(halves), 4)
    f = 4 * LANES * h[:, None] + 4 * lane[None, :] + r[:, None]
    weight = np.where(f == 0, 1.0, 2.0) / (samples * math.sqrt(channels))
    angle = (f[:, :, None] * np.arange(LANES)[None, None, :] % samples) * (2 * np.pi / samples)
    first = [weight[:, :, None] * np.cos(angle), weight[:, :, None] * np.sin(angle)]
    steps = samples // LANES
    b = 4 * lane[None, :] + np.arange(4)[:, None]
    turn = (b[:, None, :] * np.arange(steps)[None, :, None] % steps) * (2 * np.pi / steps)
    second = [np.cos(turn), np.sin(turn)]
    return [v.astype(np.float32) for v in first + second]


def member_rows(edges_ref, channel, bands, channels):
    rows = []
    for j in range(bands):
        inside = channel < (channels if j == bands - 1 else edges_ref[j])
        if j:
            inside = jnp.logical_and(inside, channel >= edges_ref[j - 1])
        rows.append(inside)
    return rows


def power_kernel(bands, channels, edges_ref, mask_ref, x_ref, out_ref, acc_ref):
    local, samples = x_ref.shape
    window = samples // NBLK
    first = lax.axis_index("wide") * local
    rows = 64

    def square(i, carry):
        at = pl.ds(pl.multiple_of(i * rows, rows), rows)
        for k in range(NBLK):
            total = None
            for p in range(window // LANES):
                v = x_ref[at, pl.ds(k * window + p * LANES, LANES)].astype(jnp.float32)
                total = v * v if total is None else total + v * v
            acc_ref[at, pl.ds(k * LANES, LANES)] = total
        return carry

    lax.fori_loop(0, local // rows, square, 0)
    channel = first + lax.broadcasted_iota(jnp.int32, (1, local), 1)
    keep = mask_ref[...].astype(jnp.float32)
    picks = [jnp.where(m, keep, 0.0) for m in member_rows(edges_ref, channel, bands, channels)]
    pick = jnp.concatenate(picks, axis=0)
    summed = jnp.dot(pick, acc_ref[...], precision=HIGH, preferred_element_type=jnp.float32)
    lane = lax.broadcasted_iota(jnp.int32, (bands, LANES), 1)
    out = jnp.zeros((bands, LANES), jnp.float32)
    for k in range(NBLK):
        part = jnp.sum(summed[:, k * LANES : (k + 1) * LANES], axis=1, keepdims=True)
        out = jnp.where(lane == k, part / window, out)
    out_ref[...] = out


def share_kernel(n, x_ref, out_ref, got, send_sem, recv_sem):
    me = lax.axis_index("wide")
    barrier = pltpu.get_barrier_semaphore()
    for step in range(1, n):
        pl.semaphore_signal(
            barrier, inc=1, device_id={"wide": lax.rem(me + step, n)}, device_id_type=MESH
        )
    pl.semaphore_wait(barrier, n - 1)
    copies = []
    for step in range(1, n):
        copy = pltpu.make_async_remote_copy(
            src_ref=x_ref,
            dst_ref=got.at[step],
            send_sem=send_sem.at[step],
            recv_sem=recv_sem.at[step],
            device_id={"wide": lax.rem(me + step, n)},
            device_id_type=MESH,
        )
        copy.start()
        copies.append(copy)
    total = x_ref[...]
    for step in range(1, n):
        copies[step - 1].wait()
        total = total + got[step]
    out_ref[...] = total


def spectrum_kernel(
    bands, channels, trials,
    edges_ref, delays_ref, mask_ref, power_ref, x_ref, ac_ref, as_ref, bc_ref, bs_ref,
    out_ref,
    tab_cos, tab_sin, y_ref, spec_re, spec_im, rot_ref, frac_ref,
):
    local, samples = x_ref.shape
    quarter = samples // 4
    window = samples // NBLK
    group = quarter // 4
    halves = group // LANES
    first = lax.axis_index("wide") * local
    fine = bc_ref.shape[0]

    def fill(i, carry):
        at = pl.ds(pl.multiple_of(i * fine, fine), fine)
        ca, sa = ac_ref[pl.ds(i, 1), :], as_ref[pl.ds(i, 1), :]
        cb, sb = bc_ref[...], bs_ref[...]
        tab_cos[at, :] = (ca * cb - sa * sb).astype(jnp.bfloat16)
        tab_sin[at, :] = (sa * cb + ca * sb).astype(jnp.bfloat16)
        return carry

    lax.fori_loop(0, quarter // fine, fill, 0)

    channel = first + lax.broadcasted_iota(jnp.int32, (local, LANES), 0)
    ratio = 0.5 + 0.5 * (channel.astype(jnp.float32) + 0.5) / channels
    fraction = (1.0 / (ratio * ratio) - 1.0) / 3.0
    frac_ref[...] = fraction
    lane = lax.broadcasted_iota(jnp.int32, (1, LANES), 1)
    delay_row = jnp.zeros((1, LANES), jnp.float32)
    for d in range(trials):
        delay_row = jnp.where(lane == d, delays_ref[d].astype(jnp.float32), delay_row)
    sweep = fraction * (delay_row * (1.0 / samples))
    rotations = cos_sin_turns(sweep) + cos_sin_turns(sweep * (4.0 * LANES))
    for d in range(trials):
        for i, rot in enumerate(rotations):
            rot_ref[d, i] = jnp.broadcast_to(rot[:, d : d + 1], (local, LANES))

    scale = jnp.zeros((local, LANES), jnp.float32)
    members = member_rows(edges_ref, channel, bands, channels)
    for j in range(bands):
        high = channels if j == bands - 1 else edges_ref[j]
        low = edges_ref[j - 1] if j else 0
        width = jnp.full((1, LANES), high - low, jnp.int32).astype(jnp.float32)
        level = 1.0 / jnp.sqrt(power_ref[j : j + 1, :] / width + 1e-05)
        scale = jnp.where(members[j], level, scale)
    scale = scale * mask_ref[...].astype(jnp.float32)

    per = quarter // window
    for h in range(per):
        columns = [scale[:, m * per + h : m * per + h + 1] for m in range(4)]
        for p in range(window // LANES):
            start = h * window + p * LANES
            x0, x1, x2, x3 = (
                x_ref[:, m * quarter + start : m * quarter + start + LANES].astype(jnp.float32)
                * columns[m]
                for m in range(4)
            )
            here = slice(start, start + LANES)
            y_ref[0, :, here] = ((x0 + x2) + (x1 + x3)).astype(jnp.bfloat16)
            y_ref[1, :, here] = ((x0 + x2) - (x1 + x3)).astype(jnp.bfloat16)
            y_ref[2, :, here] = (x0 - x2).astype(jnp.bfloat16)
            y_ref[3, :, here] = (x1 - x3).astype(jnp.bfloat16)

    def product(which, table, r):
        return jnp.dot(
            y_ref[which], table[:, r * group : (r + 1) * group], preferred_element_type=jnp.float32
        )

    def put(r, real, imag):
        spec_re[:, r * group : (r + 1) * group] = real
        spec_im[:, r * group : (r + 1) * group] = imag

    put(0, product(0, tab_cos, 0), -product(0, tab_sin, 0))
    put(2, product(1, tab_cos, 2), -product(1, tab_sin, 2))
    put(1, product(2, tab_cos, 1) - product(3, tab_sin, 1),
        -(product(2, tab_sin, 1) + product(3, tab_cos, 1)))
    put(3, product(2, tab_cos, 3) + product(3, tab_sin, 3),
        product(3, tab_cos, 3) - product(2, tab_sin, 3))

    lane_step = lax.broadcasted_iota(jnp.int32, (8, LANES), 1).astype(jnp.float32) * 4.0
    blocks = 4 * halves

    def trial(d, carry):
        delay = delays_ref[d].astype(jnp.float32) * (1.0 / samples)
        per_lane = lane_step * delay

        def rotate(i, totals):
            at = pl.ds(pl.multiple_of(i * 8, 8), 8)
            base_re, base_im = cos_sin_turns(frac_ref[at, :] * per_lane)
            one_re, one_im = rot_ref[d, 0, at, :], rot_ref[d, 1, at, :]
            far_re, far_im = rot_ref[d, 2, at, :], rot_ref[d, 3, at, :]
            totals = list(totals)
            for h in range(halves):
                e_re, e_im = base_re, base_im
                for r in range(4):
                    col = pl.ds((r * halves + h) * LANES, LANES)
                    s_re, s_im = spec_re[at, col], spec_im[at, col]
                    k = r * halves + h
                    totals[k] = totals[k] + (s_re * e_re - s_im * e_im)
                    totals[blocks + k] = totals[blocks + k] + (s_re * e_im + s_im * e_re)
                    if r < 3:
                        e_re, e_im = e_re * one_re - e_im * one_im, e_re * one_im + e_im * one_re
                if h < halves - 1:
                    base_re, base_im = (
                        base_re * far_re - base_im * far_im,
                        base_re * far_im + base_im * far_re,
                    )
            return tuple(totals)

        zero = jnp.zeros((8, LANES), jnp.float32)
        totals = lax.fori_loop(0, local // 8, rotate, (zero,) * (2 * blocks))
        out_ref[d] = jnp.concatenate([jnp.sum(v, axis=0, keepdims=True) for v in totals], axis=0)
        return carry

    lax.fori_loop(0, trials, trial, 0)


def trade_kernel(n, x_ref, out_ref, got, send_sem, recv_sem):
    me = lax.axis_index("wide")
    share = out_ref.shape[0]
    barrier = pltpu.get_barrier_semaphore()
    for step in range(1, n):
        pl.semaphore_signal(
            barrier, inc=1, device_id={"wide": lax.rem(me + step, n)}, device_id_type=MESH
        )
    pl.semaphore_wait(barrier, n - 1)
    copies = []
    for step in range(1, n):
        to = lax.rem(me + step, n)
        copy = pltpu.make_async_remote_copy(
            src_ref=x_ref.at[pl.ds(to * share, share)],
            dst_ref=got.at[step],
            send_sem=send_sem.at[step],
            recv_sem=recv_sem.at[step],
            device_id={"wide": to},
            device_id_type=MESH,
        )
        copy.start()
        copies.append(copy)
    total = x_ref[pl.ds(me * share, share)]
    for step in range(1, n):
        copies[step - 1].wait()
        total = total + got[step]
    out_ref[...] = total


def series_kernel(x_ref, fc_ref, fs_ref, gc_ref, gs_ref, out_ref):
    blocks = fc_ref.shape[0]
    halves = blocks // 4
    for b in range(x_ref.shape[0]):
        rounded = x_ref[b].astype(jnp.bfloat16).astype(jnp.float32)
        turned = jnp.transpose(rounded)
        series = None
        for r in range(4):
            re = im = None
            for h in range(halves):
                k = r * halves + h
                d_re, d_im = turned[:, k : k + 1], turned[:, blocks + k : blocks + k + 1]
                p_re = d_re * fc_ref[k] - d_im * fs_ref[k]
                p_im = d_re * fs_ref[k] + d_im * fc_ref[k]
                re = p_re if re is None else re + p_re
                im = p_im if im is None else im + p_im
            part = jnp.dot(
                gc_ref[r], re, precision=HIGH, preferred_element_type=jnp.float32
            ) - jnp.dot(gs_ref[r], im, precision=HIGH, preferred_element_type=jnp.float32)
            series = part if series is None else series + part
        out_ref[b] = series


def exchange(kernel, n, x, out_shape, slot, collective_id):
    return pl.pallas_call(
        functools.partial(kernel, n),
        out_shape=jax.ShapeDtypeStruct(out_shape, x.dtype),
        in_specs=[VMEM],
        out_specs=VMEM,
        scratch_shapes=[
            pltpu.VMEM((n,) + slot, x.dtype),
            pltpu.SemaphoreType.DMA((n,)),
            pltpu.SemaphoreType.DMA((n,)),
        ],
        compiler_params=pltpu.CompilerParams(collective_id=collective_id, has_side_effects=True),
    )(x)


def body(n, filterbank, channel_mask, band_edges, dm_delays):
    beams, local, samples = filterbank.shape
    channels = local * n
    bands = band_edges.shape[0] + 1
    trials = dm_delays.shape[0]
    share = trials // n
    quarter = samples // 4
    blocks = quarter // LANES
    steps = samples // LANES
    ac, as_, bc, bs = forward_seeds(samples)
    fc, fs, gc, gs = inverse_seeds(samples, channels)
    x = filterbank.reshape(local, samples)

    local_power = pl.pallas_call(
        functools.partial(power_kernel, bands, channels),
        out_shape=jax.ShapeDtypeStruct((bands, LANES), jnp.float32),
        in_specs=[SMEM, VMEM, VMEM],
        out_specs=VMEM,
        scratch_shapes=[pltpu.VMEM((local, NBLK * LANES), jnp.float32)],
    )(band_edges, channel_mask.reshape(1, local), x)
    band_power = exchange(
        share_kernel, n, local_power, (bands, LANES), (bands, LANES), 0
    )
    partial = pl.pallas_call(
        functools.partial(spectrum_kernel, bands, channels, trials),
        out_shape=jax.ShapeDtypeStruct((trials, 2 * blocks, LANES), jnp.float32),
        in_specs=[SMEM, SMEM] + [VMEM] * 7,
        out_specs=VMEM,
        scratch_shapes=[
            pltpu.VMEM((quarter, quarter), jnp.bfloat16),
            pltpu.VMEM((quarter, quarter), jnp.bfloat16),
            pltpu.VMEM((4, local, quarter), jnp.bfloat16),
            pltpu.VMEM((local, quarter), jnp.float32),
            pltpu.VMEM((local, quarter), jnp.float32),
            pltpu.VMEM((trials, 4, local, LANES), jnp.float32),
            pltpu.VMEM((local, LANES), jnp.float32),
        ],
    )(band_edges, dm_delays, channel_mask.reshape(local, 1), band_power, x, ac, as_, bc, bs)
    summed = exchange(
        trade_kernel, n, partial, (share, 2 * blocks, LANES), (share, 2 * blocks, LANES), 1
    )
    series = pl.pallas_call(
        series_kernel,
        out_shape=jax.ShapeDtypeStruct((share, steps, LANES), jnp.float32),
        in_specs=[VMEM] * 5,
        out_specs=VMEM,
    )(summed, fc, fs, gc, gs)
    return series.reshape(beams, share, samples)


def solution(mesh):
    return jax.shard_map(
        functools.partial(body, mesh.shape["wide"]),
        mesh=mesh,
        in_specs=(P("beam", "wide", None), P(("beam", "wide")), P(), P()),
        out_specs=P("beam", "wide", None),
        check_vma=False,
    )
```

```python
import functools
import math

import jax
import jax.numpy as jnp
import numpy as np
from jax import lax
from jax.experimental import pallas as pl
from jax.experimental.pallas import tpu as pltpu
from jax.sharding import PartitionSpec as P

NBLK = 8
LANES = 128
VMEM = pl.BlockSpec(memory_space=pltpu.VMEM)
SMEM = pl.BlockSpec(memory_space=pltpu.SMEM)
MESH = pl.DeviceIdType.MESH
HIGH = lax.Precision.HIGHEST


def turn_coefficients():
    degree = 5
    nodes = np.cos((np.arange(64) + 0.5) * np.pi / 64) * 0.125 + 0.125
    root = np.sqrt(nodes)
    cos_fit = np.polynomial.Chebyshev.fit(nodes, np.cos(2 * np.pi * root), degree, domain=[0, 0.25])
    sin_fit = np.polynomial.Chebyshev.fit(
        nodes, np.sin(2 * np.pi * root) / root, degree, domain=[0, 0.25]
    )
    as_power = lambda fit: [float(np.float32(v)) for v in fit.convert(kind=np.polynomial.Polynomial).coef]
    return as_power(cos_fit), as_power(sin_fit)


COS_COEF, SIN_COEF = turn_coefficients()


def cos_sin_turns(turns):
    r = turns - jnp.floor(turns + 0.5)
    s = r * r
    c = jnp.full_like(s, COS_COEF[-1])
    q = jnp.full_like(s, SIN_COEF[-1])
    for a, b in zip(COS_COEF[-2::-1], SIN_COEF[-2::-1]):
        c = c * s + a
        q = q * s + b
    return c, q * r


def forward_seeds(samples):
    fine = 32
    quarter = samples // 4
    f = (4 * np.arange(quarter // 4)[None, :] + np.arange(4)[:, None]).reshape(-1)
    coarse = (np.arange(quarter // fine) * fine)[:, None] * f[None, :] % samples
    small = np.arange(fine)[:, None] * f[None, :] % samples
    out = []
    for product in (coarse, small):
        angle = product * (2 * np.pi / samples)
        out += [np.cos(angle), np.sin(angle)]
    return [v.astype(np.float32) for v in out]


def inverse_seeds(samples, channels):
    halves = samples // 16 // LANES
    lane = np.arange(LANES)
    r = np.repeat(np.arange(4), halves)
    h = np.tile(np.arange(halves), 4)
    f = 4 * LANES * h[:, None] + 4 * lane[None, :] + r[:, None]
    weight = np.where(f == 0, 1.0, 2.0) / (samples * math.sqrt(channels))
    angle = (f[:, :, None] * np.arange(LANES)[None, None, :] % samples) * (2 * np.pi / samples)
    first = [weight[:, :, None] * np.cos(angle), weight[:, :, None] * np.sin(angle)]
    steps = samples // LANES
    b = 4 * lane[None, :] + np.arange(4)[:, None]
    turn = (b[:, None, :] * np.arange(steps)[None, :, None] % steps) * (2 * np.pi / steps)
    second = [np.cos(turn), np.sin(turn)]
    return [v.astype(np.float32) for v in first + second]


def member_rows(edges_ref, channel, bands, channels):
    rows = []
    for j in range(bands):
        inside = channel < (channels if j == bands - 1 else edges_ref[j])
        if j:
            inside = jnp.logical_and(inside, channel >= edges_ref[j - 1])
        rows.append(inside)
    return rows


def fused_kernel(
    n, bands, channels, trials,
    edges_ref, delays_ref, mask_ref, x_ref, ac_ref, as_ref, bc_ref, bs_ref,
    out_ref,
    acc_ref, tab_cos, tab_sin, y_ref, spec_re, spec_im, rot_ref, frac_ref,
    own_power, got_power, part_ref, got_part,
    power_send, power_recv, part_send, part_recv,
):
    local, samples = x_ref.shape
    quarter = samples // 4
    window = samples // NBLK
    group = quarter // 4
    halves = group // LANES
    share = out_ref.shape[0]
    fine = bc_ref.shape[0]
    me = lax.axis_index("wide")
    first = me * local

    barrier = pltpu.get_barrier_semaphore()
    for step in range(1, n):
        pl.semaphore_signal(
            barrier, inc=1, device_id={"wide": lax.rem(me + step, n)}, device_id_type=MESH
        )

    rows = 64

    def square(i, carry):
        at = pl.ds(pl.multiple_of(i * rows, rows), rows)
        for k in range(NBLK):
            total = None
            for p in range(window // LANES):
                v = x_ref[at, pl.ds(k * window + p * LANES, LANES)].astype(jnp.float32)
                total = v * v if total is None else total + v * v
            acc_ref[at, pl.ds(k * LANES, LANES)] = total
        return carry

    lax.fori_loop(0, local // rows, square, 0)
    channel_row = first + lax.broadcasted_iota(jnp.int32, (1, local), 1)
    keep = mask_ref[...].astype(jnp.float32)
    picks = [jnp.where(m, keep, 0.0) for m in member_rows(edges_ref, channel_row, bands, channels)]
    pick = jnp.concatenate(picks, axis=0)
    summed = jnp.dot(pick, acc_ref[...], precision=HIGH, preferred_element_type=jnp.float32)
    spot = lax.broadcasted_iota(jnp.int32, (bands, LANES), 1)
    powers = jnp.zeros((bands, LANES), jnp.float32)
    for k in range(NBLK):
        part = jnp.sum(summed[:, k * LANES : (k + 1) * LANES], axis=1, keepdims=True)
        powers = jnp.where(spot == k, part / window, powers)
    own_power[...] = powers

    channel = first + lax.broadcasted_iota(jnp.int32, (local, LANES), 0)
    ratio = 0.5 + 0.5 * (channel.astype(jnp.float32) + 0.5) / channels
    fraction = (1.0 / (ratio * ratio) - 1.0) / 3.0
    frac_ref[...] = fraction
    lane = lax.broadcasted_iota(jnp.int32, (1, LANES), 1)
    delay_row = jnp.zeros((1, LANES), jnp.float32)
    for d in range(trials):
        delay_row = jnp.where(lane == d, delays_ref[d].astype(jnp.float32), delay_row)
    sweep = fraction * (delay_row * (1.0 / samples))
    rotations = cos_sin_turns(sweep) + cos_sin_turns(sweep * (4.0 * LANES))

    pl.semaphore_wait(barrier, n - 1)
    power_copies = []
    for step in range(1, n):
        copy = pltpu.make_async_remote_copy(
            src_ref=own_power,
            dst_ref=got_power.at[step],
            send_sem=power_send.at[step],
            recv_sem=power_recv.at[step],
            device_id={"wide": lax.rem(me + step, n)},
            device_id_type=MESH,
        )
        copy.start()
        power_copies.append(copy)

    for d in range(trials):
        for i, rot in enumerate(rotations):
            rot_ref[d, i] = jnp.broadcast_to(rot[:, d : d + 1], (local, LANES))

    def fill(i, carry):
        at = pl.ds(pl.multiple_of(i * fine, fine), fine)
        ca, sa = ac_ref[pl.ds(i, 1), :], as_ref[pl.ds(i, 1), :]
        cb, sb = bc_ref[...], bs_ref[...]
        tab_cos[at, :] = (ca * cb - sa * sb).astype(jnp.bfloat16)
        tab_sin[at, :] = (sa * cb + ca * sb).astype(jnp.bfloat16)
        return carry

    lax.fori_loop(0, quarter // fine, fill, 0)

    band_power = own_power[...]
    for step in range(1, n):
        power_copies[step - 1].wait()
        band_power = band_power + got_power[step]

    scale = jnp.zeros((local, LANES), jnp.float32)
    members = member_rows(edges_ref, channel, bands, channels)
    for j in range(bands):
        high = channels if j == bands - 1 else edges_ref[j]
        low = edges_ref[j - 1] if j else 0
        width = jnp.full((1, LANES), high - low, jnp.int32).astype(jnp.float32)
        level = 1.0 / jnp.sqrt(band_power[j : j + 1, :] / width + 1e-05)
        scale = jnp.where(members[j], level, scale)
    scale = scale * jnp.transpose(jnp.broadcast_to(keep, (LANES, local)))

    per = quarter // window
    for h in range(per):
        columns = [scale[:, m * per + h : m * per + h + 1] for m in range(4)]
        for p in range(window // LANES):
            start = h * window + p * LANES
            x0, x1, x2, x3 = (
                x_ref[:, m * quarter + start : m * quarter + start + LANES].astype(jnp.float32)
                * columns[m]
                for m in range(4)
            )
            here = slice(start, start + LANES)
            y_ref[0, :, here] = ((x0 + x2) + (x1 + x3)).astype(jnp.bfloat16)
            y_ref[1, :, here] = ((x0 + x2) - (x1 + x3)).astype(jnp.bfloat16)
            y_ref[2, :, here] = (x0 - x2).astype(jnp.bfloat16)
            y_ref[3, :, here] = (x1 - x3).astype(jnp.bfloat16)

    def product(which, table, r):
        return jnp.dot(
            y_ref[which], table[:, r * group : (r + 1) * group], preferred_element_type=jnp.float32
        )

    def put(r, real, imag):
        spec_re[:, r * group : (r + 1) * group] = real
        spec_im[:, r * group : (r + 1) * group] = imag

    put(0, product(0, tab_cos, 0), -product(0, tab_sin, 0))
    put(2, product(1, tab_cos, 2), -product(1, tab_sin, 2))
    put(1, product(2, tab_cos, 1) - product(3, tab_sin, 1),
        -(product(2, tab_sin, 1) + product(3, tab_cos, 1)))
    put(3, product(2, tab_cos, 3) + product(3, tab_sin, 3),
        product(3, tab_cos, 3) - product(2, tab_sin, 3))

    lane_step = lax.broadcasted_iota(jnp.int32, (8, LANES), 1).astype(jnp.float32) * 4.0
    blocks = 4 * halves
    early = max(1, local // 32)

    def part_copy(step):
        return pltpu.make_async_remote_copy(
            src_ref=part_ref.at[step],
            dst_ref=got_part.at[step],
            send_sem=part_send.at[step],
            recv_sem=part_recv.at[step],
            device_id={"wide": lax.rem(me + step, n)},
            device_id_type=MESH,
        )

    def owner_step(step, carry):
        owner = lax.rem(me + step, n)
        for sub in range(share):
            d = owner * share + sub
            delay = delays_ref[d].astype(jnp.float32) * (1.0 / samples)
            per_lane = lane_step * delay

            def rotate(i, totals):
                at = pl.ds(pl.multiple_of(i * 8, 8), 8)
                base_re, base_im = cos_sin_turns(frac_ref[at, :] * per_lane)
                one_re, one_im = rot_ref[d, 0, at, :], rot_ref[d, 1, at, :]
                far_re, far_im = rot_ref[d, 2, at, :], rot_ref[d, 3, at, :]
                twice = one_re + one_re
                totals = list(totals)
                for h in range(halves):
                    phases = [
                        (base_re, base_im),
                        (base_re * one_re - base_im * one_im, base_re * one_im + base_im * one_re),
                    ]
                    for r in range(4):
                        if r > 1:
                            (b_re, b_im), (a_re, a_im) = phases[-2:]
                            phases.append((twice * a_re - b_re, twice * a_im - b_im))
                        e_re, e_im = phases[r]
                        k = r * halves + h
                        col = pl.ds(k * LANES, LANES)
                        s_re, s_im = spec_re[at, col], spec_im[at, col]
                        totals[k] = totals[k] + (s_re * e_re - s_im * e_im)
                        totals[blocks + k] = totals[blocks + k] + (s_re * e_im + s_im * e_re)
                    if h < halves - 1:
                        base_re, base_im = (
                            base_re * far_re - base_im * far_im,
                            base_re * far_im + base_im * far_re,
                        )
                return tuple(totals)

            zero = jnp.zeros((8, LANES), jnp.float32)
            totals = lax.fori_loop(0, early, rotate, (zero,) * (2 * blocks))
            if sub == 0:

                @pl.when(step > 1)
                def _():
                    part_copy(step - 1).start()

            totals = lax.fori_loop(early, local // 8, rotate, totals)
            part_ref[step, sub] = jnp.concatenate(
                [jnp.sum(v, axis=0, keepdims=True) for v in totals], axis=0
            )
        return carry

    lax.fori_loop(1, n + 1, owner_step, 0)
    total = part_ref[n]
    for step in range(1, n):
        part_copy(step).wait()
        total = total + got_part[step]
    out_ref[...] = total


def series_kernel(x_ref, fc_ref, fs_ref, gc_ref, gs_ref, out_ref):
    blocks = fc_ref.shape[0]
    halves = blocks // 4
    for b in range(x_ref.shape[0]):
        rounded = x_ref[b].astype(jnp.bfloat16).astype(jnp.float32)
        turned = jnp.transpose(rounded)
        series = None
        for r in range(4):
            re = im = None
            for h in range(halves):
                k = r * halves + h
                d_re, d_im = turned[:, k : k + 1], turned[:, blocks + k : blocks + k + 1]
                p_re = d_re * fc_ref[k] - d_im * fs_ref[k]
                p_im = d_re * fs_ref[k] + d_im * fc_ref[k]
                re = p_re if re is None else re + p_re
                im = p_im if im is None else im + p_im
            part = jnp.dot(
                gc_ref[r], re, precision=HIGH, preferred_element_type=jnp.float32
            ) - jnp.dot(gs_ref[r], im, precision=HIGH, preferred_element_type=jnp.float32)
            series = part if series is None else series + part
        out_ref[b] = series


def body(n, filterbank, channel_mask, band_edges, dm_delays):
    beams, local, samples = filterbank.shape
    channels = local * n
    bands = band_edges.shape[0] + 1
    trials = dm_delays.shape[0]
    share = trials // n
    quarter = samples // 4
    blocks = quarter // LANES
    steps = samples // LANES
    ac, as_, bc, bs = forward_seeds(samples)
    fc, fs, gc, gs = inverse_seeds(samples, channels)
    x = filterbank.reshape(local, samples)

    slot = (share, 2 * blocks, LANES)
    dma = pltpu.SemaphoreType.DMA((n,))
    summed = pl.pallas_call(
        functools.partial(fused_kernel, n, bands, channels, trials),
        out_shape=jax.ShapeDtypeStruct(slot, jnp.float32),
        in_specs=[SMEM, SMEM] + [VMEM] * 6,
        out_specs=VMEM,
        scratch_shapes=[
            pltpu.VMEM((local, NBLK * LANES), jnp.float32),
            pltpu.VMEM((quarter, quarter), jnp.bfloat16),
            pltpu.VMEM((quarter, quarter), jnp.bfloat16),
            pltpu.VMEM((4, local, quarter), jnp.bfloat16),
            pltpu.VMEM((local, quarter), jnp.float32),
            pltpu.VMEM((local, quarter), jnp.float32),
            pltpu.VMEM((trials, 4, local, LANES), jnp.float32),
            pltpu.VMEM((local, LANES), jnp.float32),
            pltpu.VMEM((bands, LANES), jnp.float32),
            pltpu.VMEM((n, bands, LANES), jnp.float32),
            pltpu.VMEM((n + 1,) + slot, jnp.float32),
            pltpu.VMEM((n,) + slot, jnp.float32),
            dma, dma, dma, dma,
        ],
        compiler_params=pltpu.CompilerParams(collective_id=0, has_side_effects=True),
    )(band_edges, dm_delays, channel_mask.reshape(1, local), x, ac, as_, bc, bs)
    series = pl.pallas_call(
        series_kernel,
        out_shape=jax.ShapeDtypeStruct((share, steps, LANES), jnp.float32),
        in_specs=[VMEM] * 5,
        out_specs=VMEM,
    )(summed, fc, fs, gc, gs)
    return series.reshape(beams, share, samples)


def solution(mesh):
    return jax.shard_map(
        functools.partial(body, mesh.shape["wide"]),
        mesh=mesh,
        in_specs=(P("beam", "wide", None), P(("beam", "wide")), P(), P()),
        out_specs=P("beam", "wide", None),
        check_vma=False,
    )
```

```python
import functools
import math

import jax
import jax.numpy as jnp
import numpy as np
from jax import lax
from jax.experimental import pallas as pl
from jax.experimental.pallas import tpu as pltpu
from jax.sharding import PartitionSpec as P

NBLK = 8
LANES = 128
VMEM = pl.BlockSpec(memory_space=pltpu.VMEM)
SMEM = pl.BlockSpec(memory_space=pltpu.SMEM)
MESH = pl.DeviceIdType.MESH
HIGH = lax.Precision.HIGHEST


def turn_coefficients():
    degree = 5
    nodes = np.cos((np.arange(64) + 0.5) * np.pi / 64) * 0.125 + 0.125
    root = np.sqrt(nodes)
    cos_fit = np.polynomial.Chebyshev.fit(nodes, np.cos(2 * np.pi * root), degree, domain=[0, 0.25])
    sin_fit = np.polynomial.Chebyshev.fit(
        nodes, np.sin(2 * np.pi * root) / root, degree, domain=[0, 0.25]
    )
    as_power = lambda fit: [float(np.float32(v)) for v in fit.convert(kind=np.polynomial.Polynomial).coef]
    return as_power(cos_fit), as_power(sin_fit)


COS_COEF, SIN_COEF = turn_coefficients()


def cos_sin_turns(turns):
    r = turns - jnp.floor(turns + 0.5)
    s = r * r
    c = jnp.full_like(s, COS_COEF[-1])
    q = jnp.full_like(s, SIN_COEF[-1])
    for a, b in zip(COS_COEF[-2::-1], SIN_COEF[-2::-1]):
        c = c * s + a
        q = q * s + b
    return c, q * r


def forward_seeds(samples):
    fine = 32
    quarter = samples // 4
    f = (4 * np.arange(quarter // 4)[None, :] + np.arange(4)[:, None]).reshape(-1)
    coarse = (np.arange(quarter // fine) * fine)[:, None] * f[None, :] % samples
    small = np.arange(fine)[:, None] * f[None, :] % samples
    out = []
    for product in (coarse, small):
        angle = product * (2 * np.pi / samples)
        out += [np.cos(angle), np.sin(angle)]
    return [v.astype(np.float32) for v in out]


def inverse_seeds(samples, channels):
    halves = samples // 16 // LANES
    lane = np.arange(LANES)
    r = np.repeat(np.arange(4), halves)
    h = np.tile(np.arange(halves), 4)
    f = 4 * LANES * h[:, None] + 4 * lane[None, :] + r[:, None]
    weight = np.where(f == 0, 1.0, 2.0) / (samples * math.sqrt(channels))
    angle = (f[:, :, None] * np.arange(LANES)[None, None, :] % samples) * (2 * np.pi / samples)
    first = [weight[:, :, None] * np.cos(angle), weight[:, :, None] * np.sin(angle)]
    steps = samples // LANES
    b = 4 * lane[None, :] + np.arange(4)[:, None]
    turn = (b[:, None, :] * np.arange(steps)[None, :, None] % steps) * (2 * np.pi / steps)
    second = [np.cos(turn), np.sin(turn)]
    return [v.astype(np.float32) for v in first + second]


def member_rows(edges_ref, channel, bands, channels):
    rows = []
    for j in range(bands):
        inside = channel < (channels if j == bands - 1 else edges_ref[j])
        if j:
            inside = jnp.logical_and(inside, channel >= edges_ref[j - 1])
        rows.append(inside)
    return rows


def fused_kernel(
    n, bands, channels, trials,
    edges_ref, delays_ref, mask_ref, x_ref, ac_ref, as_ref, bc_ref, bs_ref,
    out_ref,
    acc_ref, tab_cos, tab_sin, y_ref, spec_re, spec_im, rot_ref, frac_ref,
    own_power, got_power, part_ref, got_part,
    power_send, power_recv, part_send, part_recv,
):
    local, samples = x_ref.shape
    quarter = samples // 4
    window = samples // NBLK
    group = quarter // 4
    halves = group // LANES
    share = out_ref.shape[0]
    fine = bc_ref.shape[0]
    me = lax.axis_index("wide")
    first = me * local

    barrier = pltpu.get_barrier_semaphore()
    for step in range(1, n):
        pl.semaphore_signal(
            barrier, inc=1, device_id={"wide": lax.rem(me + step, n)}, device_id_type=MESH
        )

    rows = 64

    def square(i, carry):
        at = pl.ds(pl.multiple_of(i * rows, rows), rows)
        for k in range(NBLK):
            total = None
            for p in range(window // LANES):
                v = x_ref[at, pl.ds(k * window + p * LANES, LANES)].astype(jnp.float32)
                total = v * v if total is None else total + v * v
            acc_ref[at, pl.ds(k * LANES, LANES)] = total
        return carry

    lax.fori_loop(0, local // rows, square, 0)
    channel_row = first + lax.broadcasted_iota(jnp.int32, (1, local), 1)
    keep = mask_ref[...].astype(jnp.float32)
    picks = [jnp.where(m, keep, 0.0) for m in member_rows(edges_ref, channel_row, bands, channels)]
    pick = jnp.concatenate(picks, axis=0)
    summed = jnp.dot(pick, acc_ref[...], precision=HIGH, preferred_element_type=jnp.float32)
    spot = lax.broadcasted_iota(jnp.int32, (bands, LANES), 1)
    powers = jnp.zeros((bands, LANES), jnp.float32)
    for k in range(NBLK):
        part = jnp.sum(summed[:, k * LANES : (k + 1) * LANES], axis=1, keepdims=True)
        powers = jnp.where(spot == k, part / window, powers)
    own_power[...] = powers

    channel = first + lax.broadcasted_iota(jnp.int32, (local, LANES), 0)
    ratio = 0.5 + 0.5 * (channel.astype(jnp.float32) + 0.5) / channels
    fraction = (1.0 / (ratio * ratio) - 1.0) / 3.0
    frac_ref[...] = fraction
    lane = lax.broadcasted_iota(jnp.int32, (1, LANES), 1)
    delay_row = jnp.zeros((1, LANES), jnp.float32)
    for d in range(trials):
        delay_row = jnp.where(lane == d, delays_ref[d].astype(jnp.float32), delay_row)
    sweep = fraction * (delay_row * (1.0 / samples))
    rotations = cos_sin_turns(sweep) + cos_sin_turns(sweep * (4.0 * LANES))

    pl.semaphore_wait(barrier, n - 1)
    power_copies = []
    for step in range(1, n):
        copy = pltpu.make_async_remote_copy(
            src_ref=own_power,
            dst_ref=got_power.at[step],
            send_sem=power_send.at[step],
            recv_sem=power_recv.at[step],
            device_id={"wide": lax.rem(me + step, n)},
            device_id_type=MESH,
        )
        copy.start()
        power_copies.append(copy)

    for d in range(trials):
        for i, rot in enumerate(rotations):
            rot_ref[d, i] = jnp.broadcast_to(rot[:, d : d + 1], (local, LANES))

    def fill(i, carry):
        at = pl.ds(pl.multiple_of(i * fine, fine), fine)
        ca, sa = ac_ref[pl.ds(i, 1), :], as_ref[pl.ds(i, 1), :]
        cb, sb = bc_ref[...], bs_ref[...]
        tab_cos[at, :] = (ca * cb - sa * sb).astype(jnp.bfloat16)
        tab_sin[at, :] = (sa * cb + ca * sb).astype(jnp.bfloat16)
        return carry

    lax.fori_loop(0, quarter // fine, fill, 0)

    band_power = own_power[...]
    for step in range(1, n):
        power_copies[step - 1].wait()
        band_power = band_power + got_power[step]

    scale = jnp.zeros((local, LANES), jnp.float32)
    members = member_rows(edges_ref, channel, bands, channels)
    for j in range(bands):
        high = channels if j == bands - 1 else edges_ref[j]
        low = edges_ref[j - 1] if j else 0
        width = jnp.full((1, LANES), high - low, jnp.int32).astype(jnp.float32)
        level = 1.0 / jnp.sqrt(band_power[j : j + 1, :] / width + 1e-05)
        scale = jnp.where(members[j], level, scale)
    scale = scale * jnp.transpose(jnp.broadcast_to(keep, (LANES, local)))

    per = quarter // window
    for h in range(per):
        columns = [scale[:, m * per + h : m * per + h + 1] for m in range(4)]
        for p in range(window // LANES):
            start = h * window + p * LANES
            x0, x1, x2, x3 = (
                x_ref[:, m * quarter + start : m * quarter + start + LANES].astype(jnp.float32)
                * columns[m]
                for m in range(4)
            )
            here = slice(start, start + LANES)
            y_ref[0, :, here] = ((x0 + x2) + (x1 + x3)).astype(jnp.bfloat16)
            y_ref[1, :, here] = ((x0 + x2) - (x1 + x3)).astype(jnp.bfloat16)
            y_ref[2, :, here] = (x0 - x2).astype(jnp.bfloat16)
            y_ref[3, :, here] = (x1 - x3).astype(jnp.bfloat16)

    def product(which, table, r):
        return jnp.dot(
            y_ref[which], table[:, r * group : (r + 1) * group], preferred_element_type=jnp.float32
        )

    def put(r, real, imag):
        spec_re[:, r * group : (r + 1) * group] = real
        spec_im[:, r * group : (r + 1) * group] = imag

    put(0, product(0, tab_cos, 0), -product(0, tab_sin, 0))
    put(2, product(1, tab_cos, 2), -product(1, tab_sin, 2))
    put(1, product(2, tab_cos, 1) - product(3, tab_sin, 1),
        -(product(2, tab_sin, 1) + product(3, tab_cos, 1)))
    put(3, product(2, tab_cos, 3) + product(3, tab_sin, 3),
        product(3, tab_cos, 3) - product(2, tab_sin, 3))

    lane_step = lax.broadcasted_iota(jnp.int32, (8, LANES), 1).astype(jnp.float32) * 4.0
    blocks = 4 * halves
    early = max(1, local // 32)

    def part_copy(step):
        return pltpu.make_async_remote_copy(
            src_ref=part_ref.at[step],
            dst_ref=got_part.at[step],
            send_sem=part_send.at[step],
            recv_sem=part_recv.at[step],
            device_id={"wide": lax.rem(me + step, n)},
            device_id_type=MESH,
        )

    def owner_step(step, carry):
        owner = lax.rem(me + step, n)
        for sub in range(share):
            d = owner * share + sub
            delay = delays_ref[d].astype(jnp.float32) * (1.0 / samples)
            per_lane = lane_step * delay

            def rotate(i, totals):
                at = pl.ds(pl.multiple_of(i * 8, 8), 8)
                base_re, base_im = cos_sin_turns(frac_ref[at, :] * per_lane)
                one_re, one_im = rot_ref[d, 0, at, :], rot_ref[d, 1, at, :]
                far_re, far_im = rot_ref[d, 2, at, :], rot_ref[d, 3, at, :]
                twice = one_re + one_re
                totals = list(totals)
                for h in range(halves):
                    phases = [
                        (base_re, base_im),
                        (base_re * one_re - base_im * one_im, base_re * one_im + base_im * one_re),
                    ]
                    for r in range(4):
                        if r > 1:
                            (b_re, b_im), (a_re, a_im) = phases[-2:]
                            phases.append((twice * a_re - b_re, twice * a_im - b_im))
                        e_re, e_im = phases[r]
                        k = r * halves + h
                        col = pl.ds(k * LANES, LANES)
                        s_re, s_im = spec_re[at, col], spec_im[at, col]
                        totals[k] = totals[k] + (s_re * e_re - s_im * e_im)
                        totals[blocks + k] = totals[blocks + k] + (s_re * e_im + s_im * e_re)
                    if h < halves - 1:
                        base_re, base_im = (
                            base_re * far_re - base_im * far_im,
                            base_re * far_im + base_im * far_re,
                        )
                return tuple(totals)

            zero = jnp.zeros((8, LANES), jnp.float32)
            totals = lax.fori_loop(0, early, rotate, (zero,) * (2 * blocks), unroll=4)
            if sub == 0:

                @pl.when(step > 1)
                def _():
                    part_copy(step - 1).start()

            totals = lax.fori_loop(early, local // 8, rotate, totals, unroll=4)
            part_ref[step, sub] = jnp.concatenate(
                [jnp.sum(v, axis=0, keepdims=True) for v in totals], axis=0
            )
        return carry

    lax.fori_loop(1, n + 1, owner_step, 0)
    total = part_ref[n]
    for step in range(1, n):
        part_copy(step).wait()
        total = total + got_part[step]
    out_ref[...] = total


def series_kernel(x_ref, fc_ref, fs_ref, gc_ref, gs_ref, out_ref):
    blocks = fc_ref.shape[0]
    halves = blocks // 4
    for b in range(x_ref.shape[0]):
        rounded = x_ref[b].astype(jnp.bfloat16).astype(jnp.float32)
        turned = jnp.transpose(rounded)
        series = None
        for r in range(4):
            re = im = None
            for h in range(halves):
                k = r * halves + h
                d_re, d_im = turned[:, k : k + 1], turned[:, blocks + k : blocks + k + 1]
                p_re = d_re * fc_ref[k] - d_im * fs_ref[k]
                p_im = d_re * fs_ref[k] + d_im * fc_ref[k]
                re = p_re if re is None else re + p_re
                im = p_im if im is None else im + p_im
            part = jnp.dot(
                gc_ref[r], re, precision=HIGH, preferred_element_type=jnp.float32
            ) - jnp.dot(gs_ref[r], im, precision=HIGH, preferred_element_type=jnp.float32)
            series = part if series is None else series + part
        out_ref[b] = series


def body(n, filterbank, channel_mask, band_edges, dm_delays):
    beams, local, samples = filterbank.shape
    channels = local * n
    bands = band_edges.shape[0] + 1
    trials = dm_delays.shape[0]
    share = trials // n
    quarter = samples // 4
    blocks = quarter // LANES
    steps = samples // LANES
    ac, as_, bc, bs = forward_seeds(samples)
    fc, fs, gc, gs = inverse_seeds(samples, channels)
    x = filterbank.reshape(local, samples)

    slot = (share, 2 * blocks, LANES)
    dma = pltpu.SemaphoreType.DMA((n,))
    summed = pl.pallas_call(
        functools.partial(fused_kernel, n, bands, channels, trials),
        out_shape=jax.ShapeDtypeStruct(slot, jnp.float32),
        in_specs=[SMEM, SMEM] + [VMEM] * 6,
        out_specs=VMEM,
        scratch_shapes=[
            pltpu.VMEM((local, NBLK * LANES), jnp.float32),
            pltpu.VMEM((quarter, quarter), jnp.bfloat16),
            pltpu.VMEM((quarter, quarter), jnp.bfloat16),
            pltpu.VMEM((4, local, quarter), jnp.bfloat16),
            pltpu.VMEM((local, quarter), jnp.float32),
            pltpu.VMEM((local, quarter), jnp.float32),
            pltpu.VMEM((trials, 4, local, LANES), jnp.float32),
            pltpu.VMEM((local, LANES), jnp.float32),
            pltpu.VMEM((bands, LANES), jnp.float32),
            pltpu.VMEM((n, bands, LANES), jnp.float32),
            pltpu.VMEM((n + 1,) + slot, jnp.float32),
            pltpu.VMEM((n,) + slot, jnp.float32),
            dma, dma, dma, dma,
        ],
        compiler_params=pltpu.CompilerParams(collective_id=0, has_side_effects=True),
    )(band_edges, dm_delays, channel_mask.reshape(1, local), x, ac, as_, bc, bs)
    series = pl.pallas_call(
        series_kernel,
        out_shape=jax.ShapeDtypeStruct((share, steps, LANES), jnp.float32),
        in_specs=[VMEM] * 5,
        out_specs=VMEM,
    )(summed, fc, fs, gc, gs)
    return series.reshape(beams, share, samples)


def solution(mesh):
    return jax.shard_map(
        functools.partial(body, mesh.shape["wide"]),
        mesh=mesh,
        in_specs=(P("beam", "wide", None), P(("beam", "wide")), P(), P()),
        out_specs=P("beam", "wide", None),
        check_vma=False,
    )
```

```python
import functools
import math

import jax
import jax.numpy as jnp
import numpy as np
from jax import lax
from jax.experimental import pallas as pl
from jax.experimental.pallas import tpu as pltpu
from jax.sharding import PartitionSpec as P

NBLK = 8
LANES = 128
VMEM = pl.BlockSpec(memory_space=pltpu.VMEM)
SMEM = pl.BlockSpec(memory_space=pltpu.SMEM)
MESH = pl.DeviceIdType.MESH
HIGH = lax.Precision.HIGHEST


def turn_coefficients():
    degree = 5
    nodes = np.cos((np.arange(64) + 0.5) * np.pi / 64) * 0.125 + 0.125
    root = np.sqrt(nodes)
    cos_fit = np.polynomial.Chebyshev.fit(nodes, np.cos(2 * np.pi * root), degree, domain=[0, 0.25])
    sin_fit = np.polynomial.Chebyshev.fit(
        nodes, np.sin(2 * np.pi * root) / root, degree, domain=[0, 0.25]
    )
    as_power = lambda fit: [float(np.float32(v)) for v in fit.convert(kind=np.polynomial.Polynomial).coef]
    return as_power(cos_fit), as_power(sin_fit)


COS_COEF, SIN_COEF = turn_coefficients()


def cos_sin_turns(turns):
    r = turns - jnp.floor(turns + 0.5)
    s = r * r
    c = jnp.full_like(s, COS_COEF[-1])
    q = jnp.full_like(s, SIN_COEF[-1])
    for a, b in zip(COS_COEF[-2::-1], SIN_COEF[-2::-1]):
        c = c * s + a
        q = q * s + b
    return c, q * r


def forward_seeds(samples):
    fine = 32
    quarter = samples // 4
    f = (4 * np.arange(quarter // 4)[None, :] + np.arange(4)[:, None]).reshape(-1)
    coarse = (np.arange(quarter // fine) * fine)[:, None] * f[None, :] % samples
    small = np.arange(fine)[:, None] * f[None, :] % samples
    out = []
    for product in (coarse, small):
        angle = product * (2 * np.pi / samples)
        out += [np.cos(angle), np.sin(angle)]
    return [v.astype(np.float32) for v in out]


def inverse_seeds(samples, channels):
    halves = samples // 16 // LANES
    lane = np.arange(LANES)
    r = np.repeat(np.arange(4), halves)
    h = np.tile(np.arange(halves), 4)
    f = 4 * LANES * h[:, None] + 4 * lane[None, :] + r[:, None]
    weight = np.where(f == 0, 1.0, 2.0) / (samples * math.sqrt(channels))
    angle = (f[:, :, None] * np.arange(LANES)[None, None, :] % samples) * (2 * np.pi / samples)
    first = [weight[:, :, None] * np.cos(angle), weight[:, :, None] * np.sin(angle)]
    steps = samples // LANES
    b = 4 * lane[None, :] + np.arange(4)[:, None]
    turn = (b[:, None, :] * np.arange(steps)[None, :, None] % steps) * (2 * np.pi / steps)
    second = np.stack([np.cos(turn), -np.sin(turn)], axis=1).reshape(8, steps, LANES)
    second = np.concatenate(list(second), axis=1)
    return [v.astype(np.float32) for v in first + [second]]


def member_rows(edges_ref, channel, bands, channels):
    rows = []
    for j in range(bands):
        inside = channel < (channels if j == bands - 1 else edges_ref[j])
        if j:
            inside = jnp.logical_and(inside, channel >= edges_ref[j - 1])
        rows.append(inside)
    return rows


def partner(me, step, n):
    if n & (n - 1):
        return lax.rem(me + step, n)
    out, bit = 0, 1
    while bit < n:
        out = out + lax.rem(me // bit + step // bit, 2) * bit
        bit *= 2
    return out


def fused_kernel(
    n, bands, channels, trials,
    edges_ref, delays_ref, mask_ref, x_hbm, ac_ref, as_ref, bc_ref, bs_ref,
    out_ref,
    x_ref, acc_ref, tab_cos, tab_sin, y_ref, spec_re, spec_im, rot_ref, base_ref, frac_ref,
    own_power, got_power, part_ref, got_part,
    x_sem, power_send, power_recv, part_send, part_recv,
):
    local, samples = x_ref.shape
    quarter = samples // 4
    window = samples // NBLK
    group = quarter // 4
    halves = group // LANES
    share = out_ref.shape[0]
    fine = bc_ref.shape[0]
    me = lax.axis_index("wide")
    first = me * local

    barrier = pltpu.get_barrier_semaphore()
    for step in range(1, n):
        pl.semaphore_signal(
            barrier, inc=1, device_id={"wide": lax.rem(me + step, n)}, device_id_type=MESH
        )

    rows = 64

    def load(i):
        at = pl.ds(pl.multiple_of(i * rows, rows), rows)
        return pltpu.make_async_copy(x_hbm.at[at], x_ref.at[at], x_sem.at[i])

    for i in range(local // rows):
        load(i).start()

    def fill(i, carry):
        at = pl.ds(pl.multiple_of(i * fine, fine), fine)
        ca, sa = ac_ref[pl.ds(i, 1), :], as_ref[pl.ds(i, 1), :]
        cb, sb = bc_ref[...], bs_ref[...]
        tab_cos[at, :] = (ca * cb - sa * sb).astype(jnp.bfloat16)
        tab_sin[at, :] = (sa * cb + ca * sb).astype(jnp.bfloat16)
        return carry

    lax.fori_loop(0, quarter // fine, fill, 0)

    def square(i, carry):
        load(i).wait()
        at = pl.ds(pl.multiple_of(i * rows, rows), rows)
        for k in range(NBLK):
            total = None
            for p in range(window // LANES):
                v = x_ref[at, pl.ds(k * window + p * LANES, LANES)].astype(jnp.float32)
                total = v * v if total is None else total + v * v
            acc_ref[at, pl.ds(k * LANES, LANES)] = total
        return carry

    lax.fori_loop(0, local // rows, square, 0)
    channel_row = first + lax.broadcasted_iota(jnp.int32, (1, local), 1)
    keep = mask_ref[...].astype(jnp.float32)
    picks = [jnp.where(m, keep, 0.0) for m in member_rows(edges_ref, channel_row, bands, channels)]
    pick = jnp.concatenate(picks, axis=0)
    summed = jnp.dot(pick, acc_ref[...], precision=HIGH, preferred_element_type=jnp.float32)
    spot = lax.broadcasted_iota(jnp.int32, (bands, LANES), 1)
    powers = jnp.zeros((bands, LANES), jnp.float32)
    for k in range(NBLK):
        part = jnp.sum(summed[:, k * LANES : (k + 1) * LANES], axis=1, keepdims=True)
        powers = jnp.where(spot == k, part / window, powers)
    own_power[...] = powers

    channel = first + lax.broadcasted_iota(jnp.int32, (local, LANES), 0)
    ratio = 0.5 + 0.5 * (channel.astype(jnp.float32) + 0.5) / channels
    fraction = (1.0 / (ratio * ratio) - 1.0) / 3.0
    frac_ref[...] = fraction
    lane = lax.broadcasted_iota(jnp.int32, (1, LANES), 1)
    delay_row = jnp.zeros((1, LANES), jnp.float32)
    for d in range(trials):
        delay_row = jnp.where(lane == d, delays_ref[d].astype(jnp.float32), delay_row)
    sweep = fraction * (delay_row * (1.0 / samples))
    rotations = cos_sin_turns(sweep) + cos_sin_turns(sweep * (4.0 * LANES))

    pl.semaphore_wait(barrier, n - 1)
    power_copies = []
    for step in range(1, n):
        copy = pltpu.make_async_remote_copy(
            src_ref=own_power,
            dst_ref=got_power.at[step],
            send_sem=power_send.at[step],
            recv_sem=power_recv.at[step],
            device_id={"wide": lax.rem(me + step, n)},
            device_id_type=MESH,
        )
        copy.start()
        power_copies.append(copy)

    for d in range(trials):
        for i, rot in enumerate(rotations):
            rot_ref[d, i] = jnp.broadcast_to(rot[:, d : d + 1], (local, LANES))

    def base(d, carry):
        delay = delays_ref[d].astype(jnp.float32) * (1.0 / samples)
        per_lane = lane_step * delay

        def tile(i, inner):
            at = pl.ds(pl.multiple_of(i * 8, 8), 8)
            base_ref[d, 0, at, :], base_ref[d, 1, at, :] = cos_sin_turns(frac_ref[at, :] * per_lane)
            return inner

        return lax.fori_loop(0, local // 8, tile, carry, unroll=8)

    lane_step = lax.broadcasted_iota(jnp.int32, (8, LANES), 1).astype(jnp.float32) * 4.0
    lax.fori_loop(0, trials, base, 0)

    band_power = own_power[...]
    for step in range(1, n):
        power_copies[step - 1].wait()
        band_power = band_power + got_power[step]

    scale = jnp.zeros((local, LANES), jnp.float32)
    members = member_rows(edges_ref, channel, bands, channels)
    for j in range(bands):
        high = channels if j == bands - 1 else edges_ref[j]
        low = edges_ref[j - 1] if j else 0
        width = jnp.full((1, LANES), high - low, jnp.int32).astype(jnp.float32)
        level = 1.0 / jnp.sqrt(band_power[j : j + 1, :] / width + 1e-05)
        scale = jnp.where(members[j], level, scale)
    scale = scale * jnp.transpose(jnp.broadcast_to(keep, (LANES, local)))

    per = quarter // window
    for h in range(per):
        columns = [scale[:, m * per + h : m * per + h + 1] for m in range(4)]
        for p in range(window // LANES):
            start = h * window + p * LANES
            x0, x1, x2, x3 = (
                x_ref[:, m * quarter + start : m * quarter + start + LANES].astype(jnp.float32)
                * columns[m]
                for m in range(4)
            )
            here = slice(start, start + LANES)
            y_ref[0, :, here] = ((x0 + x2) + (x1 + x3)).astype(jnp.bfloat16)
            y_ref[1, :, here] = ((x0 + x2) - (x1 + x3)).astype(jnp.bfloat16)
            y_ref[2, :, here] = (x0 - x2).astype(jnp.bfloat16)
            y_ref[3, :, here] = (x1 - x3).astype(jnp.bfloat16)

    def product(which, table, r):
        return jnp.dot(
            y_ref[which], table[:, r * group : (r + 1) * group], preferred_element_type=jnp.float32
        )

    def put(r, real, imag):
        spec_re[:, r * group : (r + 1) * group] = real
        spec_im[:, r * group : (r + 1) * group] = imag

    put(0, product(0, tab_cos, 0), -product(0, tab_sin, 0))
    put(2, product(1, tab_cos, 2), -product(1, tab_sin, 2))
    put(1, product(2, tab_cos, 1) - product(3, tab_sin, 1),
        -(product(2, tab_sin, 1) + product(3, tab_cos, 1)))
    put(3, product(2, tab_cos, 3) + product(3, tab_sin, 3),
        product(3, tab_cos, 3) - product(2, tab_sin, 3))

    blocks = 4 * halves
    early = max(1, local // 32)

    def part_copy(step):
        return pltpu.make_async_remote_copy(
            src_ref=part_ref.at[step],
            dst_ref=got_part.at[step],
            send_sem=part_send.at[step],
            recv_sem=part_recv.at[step],
            device_id={"wide": partner(me, step, n)},
            device_id_type=MESH,
        )

    def owner_step(turn, carry):
        step = n - 1 - turn
        owner = partner(me, step, n)
        for sub in range(share):
            d = owner * share + sub

            def rotate(i, totals):
                at = pl.ds(pl.multiple_of(i * 8, 8), 8)
                base_re, base_im = base_ref[d, 0, at, :], base_ref[d, 1, at, :]
                one_re, one_im = rot_ref[d, 0, at, :], rot_ref[d, 1, at, :]
                far_re, far_im = rot_ref[d, 2, at, :], rot_ref[d, 3, at, :]
                twice = one_re + one_re
                totals = list(totals)
                for h in range(halves):
                    phases = [
                        (base_re, base_im),
                        (base_re * one_re - base_im * one_im, base_re * one_im + base_im * one_re),
                    ]
                    for r in range(4):
                        if r > 1:
                            (b_re, b_im), (a_re, a_im) = phases[-2:]
                            phases.append((twice * a_re - b_re, twice * a_im - b_im))
                        e_re, e_im = phases[r]
                        k = r * halves + h
                        col = pl.ds(k * LANES, LANES)
                        s_re, s_im = spec_re[at, col], spec_im[at, col]
                        totals[k] = totals[k] + (s_re * e_re - s_im * e_im)
                        totals[blocks + k] = totals[blocks + k] + (s_re * e_im + s_im * e_re)
                    if h < halves - 1:
                        base_re, base_im = (
                            base_re * far_re - base_im * far_im,
                            base_re * far_im + base_im * far_re,
                        )
                return tuple(totals)

            zero = jnp.zeros((8, LANES), jnp.float32)
            totals = lax.fori_loop(0, early, rotate, (zero,) * (2 * blocks), unroll=4)
            if sub == 0:

                @pl.when(turn > 0)
                def _():
                    part_copy(step + 1).start()

            totals = lax.fori_loop(early, local // 8, rotate, totals, unroll=4)
            part_ref[step, sub] = jnp.concatenate(
                [jnp.sum(v, axis=0, keepdims=True) for v in totals], axis=0
            )
        return carry

    lax.fori_loop(0, n, owner_step, 0)
    total = part_ref[0]
    for step in range(n - 1, 0, -1):
        part_copy(step).wait()
        total = total + got_part[step]
    out_ref[...] = total


def series_kernel(x_ref, fc_ref, fs_ref, g_ref, out_ref):
    blocks = fc_ref.shape[0]
    halves = blocks // 4
    for b in range(x_ref.shape[0]):
        rounded = x_ref[b].astype(jnp.bfloat16).astype(jnp.float32)
        turned = jnp.transpose(rounded)
        parts = []
        for r in range(4):
            re = im = None
            for h in range(halves):
                k = r * halves + h
                d_re, d_im = turned[:, k : k + 1], turned[:, blocks + k : blocks + k + 1]
                p_re = d_re * fc_ref[k] - d_im * fs_ref[k]
                p_im = d_re * fs_ref[k] + d_im * fc_ref[k]
                re = p_re if re is None else re + p_re
                im = p_im if im is None else im + p_im
            parts += [re, im]
        out_ref[b] = jnp.dot(
            g_ref[...], jnp.concatenate(parts, axis=0),
            precision=HIGH, preferred_element_type=jnp.float32,
        )


def body(n, filterbank, channel_mask, band_edges, dm_delays):
    beams, local, samples = filterbank.shape
    channels = local * n
    bands = band_edges.shape[0] + 1
    trials = dm_delays.shape[0]
    share = trials // n
    quarter = samples // 4
    blocks = quarter // LANES
    steps = samples // LANES
    ac, as_, bc, bs = forward_seeds(samples)
    fc, fs, g = inverse_seeds(samples, channels)
    x = filterbank.reshape(local, samples)

    slot = (share, 2 * blocks, LANES)
    dma = pltpu.SemaphoreType.DMA((n,))
    summed = pl.pallas_call(
        functools.partial(fused_kernel, n, bands, channels, trials),
        out_shape=jax.ShapeDtypeStruct(slot, jnp.float32),
        in_specs=[SMEM, SMEM, VMEM, pl.BlockSpec(memory_space=pl.ANY)] + [VMEM] * 4,
        out_specs=VMEM,
        scratch_shapes=[
            pltpu.VMEM((local, samples), x.dtype),
            pltpu.VMEM((local, NBLK * LANES), jnp.float32),
            pltpu.VMEM((quarter, quarter), jnp.bfloat16),
            pltpu.VMEM((quarter, quarter), jnp.bfloat16),
            pltpu.VMEM((4, local, quarter), jnp.bfloat16),
            pltpu.VMEM((local, quarter), jnp.float32),
            pltpu.VMEM((local, quarter), jnp.float32),
            pltpu.VMEM((trials, 4, local, LANES), jnp.float32),
            pltpu.VMEM((trials, 2, local, LANES), jnp.float32),
            pltpu.VMEM((local, LANES), jnp.float32),
            pltpu.VMEM((bands, LANES), jnp.float32),
            pltpu.VMEM((n, bands, LANES), jnp.float32),
            pltpu.VMEM((n,) + slot, jnp.float32),
            pltpu.VMEM((n,) + slot, jnp.float32),
            pltpu.SemaphoreType.DMA((local // 64,)), dma, dma, dma, dma,
        ],
        compiler_params=pltpu.CompilerParams(collective_id=0, has_side_effects=True),
    )(band_edges, dm_delays, channel_mask.reshape(1, local), x, ac, as_, bc, bs)
    series = pl.pallas_call(
        series_kernel,
        out_shape=jax.ShapeDtypeStruct((share, steps, LANES), jnp.float32),
        in_specs=[VMEM] * 4,
        out_specs=VMEM,
    )(summed, fc, fs, g)
    return series.reshape(beams, share, samples)


def solution(mesh):
    return jax.shard_map(
        functools.partial(body, mesh.shape["wide"]),
        mesh=mesh,
        in_specs=(P("beam", "wide", None), P(("beam", "wide")), P(), P()),
        out_specs=P("beam", "wide", None),
        check_vma=False,
    )
```

```python
import functools
import math

import jax
import jax.numpy as jnp
import numpy as np
from jax import lax
from jax.experimental import pallas as pl
from jax.experimental.pallas import tpu as pltpu
from jax.sharding import PartitionSpec as P

NBLK = 8
LANES = 128
VMEM = pl.BlockSpec(memory_space=pltpu.VMEM)
SMEM = pl.BlockSpec(memory_space=pltpu.SMEM)
MESH = pl.DeviceIdType.MESH
HIGH = lax.Precision.HIGHEST


def turn_coefficients():
    degree = 5
    nodes = np.cos((np.arange(64) + 0.5) * np.pi / 64) * 0.125 + 0.125
    root = np.sqrt(nodes)
    cos_fit = np.polynomial.Chebyshev.fit(nodes, np.cos(2 * np.pi * root), degree, domain=[0, 0.25])
    sin_fit = np.polynomial.Chebyshev.fit(
        nodes, np.sin(2 * np.pi * root) / root, degree, domain=[0, 0.25]
    )
    as_power = lambda fit: [float(np.float32(v)) for v in fit.convert(kind=np.polynomial.Polynomial).coef]
    return as_power(cos_fit), as_power(sin_fit)


COS_COEF, SIN_COEF = turn_coefficients()


def cos_sin_turns(turns):
    r = turns - jnp.floor(turns + 0.5)
    s = r * r
    c = jnp.full_like(s, COS_COEF[-1])
    q = jnp.full_like(s, SIN_COEF[-1])
    for a, b in zip(COS_COEF[-2::-1], SIN_COEF[-2::-1]):
        c = c * s + a
        q = q * s + b
    return c, q * r


def forward_seeds(samples):
    fine = 32
    quarter = samples // 4
    f = (8 * np.arange(quarter // 8)[None, :] + np.arange(8)[:, None]).reshape(-1)
    coarse = (np.arange(samples // 8 // fine) * fine)[:, None] * f[None, :] % samples
    small = np.arange(fine)[:, None] * f[None, :] % samples
    out = []
    for product in (coarse, small):
        angle = product * (2 * np.pi / samples)
        out += [np.cos(angle), np.sin(angle)]
    return [v.astype(np.float32) for v in out]


def inverse_seeds(samples, channels):
    lane = np.arange(LANES)
    f = 8 * lane[None, :] + np.arange(8)[:, None]
    weight = np.where(f == 0, 1.0, 2.0) / (samples * math.sqrt(channels))
    angle = (f[:, :, None] * np.arange(LANES)[None, None, :] % samples) * (2 * np.pi / samples)
    first = [weight[:, :, None] * np.cos(angle), weight[:, :, None] * np.sin(angle)]
    steps = samples // LANES
    b = f
    turn = (b[:, None, :] * np.arange(steps)[None, :, None] % steps) * (2 * np.pi / steps)
    second = np.stack([np.cos(turn), -np.sin(turn)], axis=1).reshape(16, steps, LANES)
    second = np.concatenate(list(second), axis=1)
    return [v.astype(np.float32) for v in first + [second]]


def member_rows(edges_ref, channel, bands, channels):
    rows = []
    for j in range(bands):
        inside = channel < (channels if j == bands - 1 else edges_ref[j])
        if j:
            inside = jnp.logical_and(inside, channel >= edges_ref[j - 1])
        rows.append(inside)
    return rows


def partner(me, step, n):
    if n & (n - 1):
        return lax.rem(me + step, n)
    out, bit = 0, 1
    while bit < n:
        out = out + lax.rem(me // bit + step // bit, 2) * bit
        bit *= 2
    return out


def fused_kernel(
    n, bands, channels, trials,
    edges_ref, delays_ref, mask_ref, x_hbm, ac_ref, as_ref, bc_ref, bs_ref,
    out_ref,
    x_ref, acc_ref, tab_ref, y_ref, spec_re, spec_im, rot_ref, base_ref, frac_ref,
    own_power, got_power, part_ref, got_part,
    x_sem, power_send, power_recv, part_send, part_recv,
):
    local, samples = x_ref.shape
    quarter = samples // 4
    window = samples // NBLK
    eighth = samples // 8
    group = quarter // 8
    assert group == LANES and eighth == window
    share = out_ref.shape[0]
    fine = bc_ref.shape[0]
    me = lax.axis_index("wide")
    first = me * local

    barrier = pltpu.get_barrier_semaphore()
    for step in range(1, n):
        pl.semaphore_signal(
            barrier, inc=1, device_id={"wide": lax.rem(me + step, n)}, device_id_type=MESH
        )

    rows = 64

    def load(i):
        at = pl.ds(pl.multiple_of(i * rows, rows), rows)
        return pltpu.make_async_copy(x_hbm.at[at], x_ref.at[at], x_sem.at[i])

    for i in range(local // rows):
        load(i).start()

    def fill(i, carry):
        at = pl.ds(pl.multiple_of(i * fine, fine), fine)
        ca, sa = ac_ref[pl.ds(i, 1), :], as_ref[pl.ds(i, 1), :]
        cb, sb = bc_ref[...], bs_ref[...]
        cos_part = (ca * cb - sa * sb).astype(jnp.bfloat16)
        sin_part = (sa * cb + ca * sb).astype(jnp.bfloat16)
        for r in range(8):
            tab_ref[at, 2 * r * group : (2 * r + 1) * group] = cos_part[:, r * group : (r + 1) * group]
            tab_ref[at, (2 * r + 1) * group : (2 * r + 2) * group] = sin_part[:, r * group : (r + 1) * group]
        return carry

    lax.fori_loop(0, eighth // fine, fill, 0)

    def square(i, carry):
        load(i).wait()
        at = pl.ds(pl.multiple_of(i * rows, rows), rows)
        for k in range(NBLK):
            total = None
            for p in range(window // LANES):
                v = x_ref[at, pl.ds(k * window + p * LANES, LANES)].astype(jnp.float32)
                total = v * v if total is None else total + v * v
            acc_ref[at, pl.ds(k * LANES, LANES)] = total
        return carry

    lax.fori_loop(0, local // rows, square, 0)
    channel_row = first + lax.broadcasted_iota(jnp.int32, (1, local), 1)
    keep = mask_ref[...].astype(jnp.float32)
    picks = [jnp.where(m, keep, 0.0) for m in member_rows(edges_ref, channel_row, bands, channels)]
    pick = jnp.concatenate(picks, axis=0)
    summed = jnp.dot(pick, acc_ref[...], precision=HIGH, preferred_element_type=jnp.float32)
    spot = lax.broadcasted_iota(jnp.int32, (bands, LANES), 1)
    powers = jnp.zeros((bands, LANES), jnp.float32)
    for k in range(NBLK):
        part = jnp.sum(summed[:, k * LANES : (k + 1) * LANES], axis=1, keepdims=True)
        powers = jnp.where(spot == k, part / window, powers)
    own_power[...] = powers

    channel = first + lax.broadcasted_iota(jnp.int32, (local, LANES), 0)
    ratio = 0.5 + 0.5 * (channel.astype(jnp.float32) + 0.5) / channels
    fraction = (1.0 / (ratio * ratio) - 1.0) / 3.0
    frac_ref[...] = fraction
    lane = lax.broadcasted_iota(jnp.int32, (1, LANES), 1)
    delay_row = jnp.zeros((1, LANES), jnp.float32)
    for d in range(trials):
        delay_row = jnp.where(lane == d, delays_ref[d].astype(jnp.float32), delay_row)
    sweep = fraction * (delay_row * (1.0 / samples))
    rotations = cos_sin_turns(sweep)

    pl.semaphore_wait(barrier, n - 1)
    power_copies = []
    for step in range(1, n):
        copy = pltpu.make_async_remote_copy(
            src_ref=own_power,
            dst_ref=got_power.at[step],
            send_sem=power_send.at[step],
            recv_sem=power_recv.at[step],
            device_id={"wide": lax.rem(me + step, n)},
            device_id_type=MESH,
        )
        copy.start()
        power_copies.append(copy)

    for d in range(trials):
        for i, rot in enumerate(rotations):
            rot_ref[d, i] = jnp.broadcast_to(rot[:, d : d + 1], (local, LANES))

    def base(d, carry):
        delay = delays_ref[d].astype(jnp.float32) * (1.0 / samples)
        per_lane = lane_step * delay

        def tile(i, inner):
            at = pl.ds(pl.multiple_of(i * 8, 8), 8)
            base_ref[d, 0, at, :], base_ref[d, 1, at, :] = cos_sin_turns(frac_ref[at, :] * per_lane)
            return inner

        return lax.fori_loop(0, local // 8, tile, carry, unroll=8)

    lane_step = lax.broadcasted_iota(jnp.int32, (8, LANES), 1).astype(jnp.float32) * 8.0
    lax.fori_loop(0, trials, base, 0)

    band_power = own_power[...]
    for step in range(1, n):
        power_copies[step - 1].wait()
        band_power = band_power + got_power[step]

    scale = jnp.zeros((local, LANES), jnp.float32)
    members = member_rows(edges_ref, channel, bands, channels)
    for j in range(bands):
        high = channels if j == bands - 1 else edges_ref[j]
        low = edges_ref[j - 1] if j else 0
        width = jnp.full((1, LANES), high - low, jnp.int32).astype(jnp.float32)
        level = 1.0 / jnp.sqrt(band_power[j : j + 1, :] / width + 1e-05)
        scale = jnp.where(members[j], level, scale)
    scale = scale * jnp.transpose(jnp.broadcast_to(keep, (LANES, local)))

    columns = [scale[:, m : m + 1] for m in range(8)]
    root = math.sqrt(0.5)
    for p in range(window // LANES):
        here = slice(p * LANES, (p + 1) * LANES)
        x = [
            x_ref[:, m * window + p * LANES : m * window + (p + 1) * LANES].astype(jnp.float32)
            * columns[m]
            for m in range(8)
        ]
        plus = [x[m] + x[m + 4] for m in range(4)]
        minus = [x[m] - x[m + 4] for m in range(4)]
        even, odd = plus[0] + plus[2], plus[1] + plus[3]
        near, far = root * (minus[1] - minus[3]), root * (minus[1] + minus[3])
        folded = (
            even + odd, even - odd,
            minus[0] + near, -(far + minus[2]),
            plus[0] - plus[2], plus[3] - plus[1],
            minus[0] - near, minus[2] - far,
        )
        for i, value in enumerate(folded):
            y_ref[i, :, here] = value.astype(jnp.bfloat16)

    def product(which, r):
        both = jnp.dot(
            y_ref[which], tab_ref[:, 2 * r * group : (2 * r + 2) * group],
            preferred_element_type=jnp.float32,
        )
        return both[:, :group], both[:, group:]

    for r in range(8):
        to = slice(r * group, (r + 1) * group)
        if r % 4 == 0:
            c, q = product(r // 4, r)
            spec_re[:, to], spec_im[:, to] = c, -q
        else:
            kind = min(r, 8 - r)
            (a_c, a_s), (b_c, b_s) = product(2 * kind, r), product(2 * kind + 1, r)
            if r < 4:
                spec_re[:, to], spec_im[:, to] = a_c + b_s, b_c - a_s
            else:
                spec_re[:, to], spec_im[:, to] = a_c - b_s, -(b_c + a_s)

    blocks = 8
    early = max(1, local // 32)

    def part_copy(step):
        return pltpu.make_async_remote_copy(
            src_ref=part_ref.at[step],
            dst_ref=got_part.at[step],
            send_sem=part_send.at[step],
            recv_sem=part_recv.at[step],
            device_id={"wide": partner(me, step, n)},
            device_id_type=MESH,
        )

    def owner_step(turn, carry):
        step = n - 1 - turn
        owner = partner(me, step, n)
        for sub in range(share):
            d = owner * share + sub

            def rotate(i, totals):
                at = pl.ds(pl.multiple_of(i * 8, 8), 8)
                base_re, base_im = base_ref[d, 0, at, :], base_ref[d, 1, at, :]
                one_re, one_im = rot_ref[d, 0, at, :], rot_ref[d, 1, at, :]
                twice = one_re + one_re
                totals = list(totals)
                phases = [
                    (base_re, base_im),
                    (base_re * one_re - base_im * one_im, base_re * one_im + base_im * one_re),
                ]
                for r in range(8):
                    if r > 1:
                        (b_re, b_im), (a_re, a_im) = phases[-2:]
                        phases.append((twice * a_re - b_re, twice * a_im - b_im))
                    e_re, e_im = phases[r]
                    col = pl.ds(r * LANES, LANES)
                    s_re, s_im = spec_re[at, col], spec_im[at, col]
                    totals[r] = totals[r] + (s_re * e_re - s_im * e_im)
                    totals[blocks + r] = totals[blocks + r] + (s_re * e_im + s_im * e_re)
                return tuple(totals)

            zero = jnp.zeros((8, LANES), jnp.float32)
            totals = lax.fori_loop(0, early, rotate, (zero,) * (2 * blocks), unroll=8)
            if sub == 0:

                @pl.when(turn > 0)
                def _():
                    part_copy(step + 1).start()

            totals = lax.fori_loop(early, local // 8, rotate, totals, unroll=8)
            part_ref[step, sub] = jnp.concatenate(
                [jnp.sum(v, axis=0, keepdims=True) for v in totals], axis=0
            )
        return carry

    lax.fori_loop(0, n, owner_step, 0)
    total = part_ref[0]
    for step in range(n - 1, 0, -1):
        part_copy(step).wait()
        total = total + got_part[step]
    out_ref[...] = total


def series_kernel(x_ref, fc_ref, fs_ref, g_ref, out_ref):
    blocks = fc_ref.shape[0]
    for b in range(x_ref.shape[0]):
        rounded = x_ref[b].astype(jnp.bfloat16).astype(jnp.float32)
        turned = jnp.transpose(rounded)
        parts = []
        for k in range(blocks):
            d_re, d_im = turned[:, k : k + 1], turned[:, blocks + k : blocks + k + 1]
            parts += [d_re * fc_ref[k] - d_im * fs_ref[k], d_re * fs_ref[k] + d_im * fc_ref[k]]
        out_ref[b] = jnp.dot(
            g_ref[...], jnp.concatenate(parts, axis=0),
            precision=HIGH, preferred_element_type=jnp.float32,
        )


def body(n, filterbank, channel_mask, band_edges, dm_delays):
    beams, local, samples = filterbank.shape
    channels = local * n
    bands = band_edges.shape[0] + 1
    trials = dm_delays.shape[0]
    share = trials // n
    quarter = samples // 4
    blocks = quarter // LANES
    steps = samples // LANES
    ac, as_, bc, bs = forward_seeds(samples)
    fc, fs, g = inverse_seeds(samples, channels)
    x = filterbank.reshape(local, samples)

    slot = (share, 2 * blocks, LANES)
    dma = pltpu.SemaphoreType.DMA((n,))
    summed = pl.pallas_call(
        functools.partial(fused_kernel, n, bands, channels, trials),
        out_shape=jax.ShapeDtypeStruct(slot, jnp.float32),
        in_specs=[SMEM, SMEM, VMEM, pl.BlockSpec(memory_space=pl.ANY)] + [VMEM] * 4,
        out_specs=VMEM,
        scratch_shapes=[
            pltpu.VMEM((local, samples), x.dtype),
            pltpu.VMEM((local, NBLK * LANES), jnp.float32),
            pltpu.VMEM((samples // 8, 2 * quarter), jnp.bfloat16),
            pltpu.VMEM((8, local, samples // 8), jnp.bfloat16),
            pltpu.VMEM((local, quarter), jnp.float32),
            pltpu.VMEM((local, quarter), jnp.float32),
            pltpu.VMEM((trials, 2, local, LANES), jnp.float32),
            pltpu.VMEM((trials, 2, local, LANES), jnp.float32),
            pltpu.VMEM((local, LANES), jnp.float32),
            pltpu.VMEM((bands, LANES), jnp.float32),
            pltpu.VMEM((n, bands, LANES), jnp.float32),
            pltpu.VMEM((n,) + slot, jnp.float32),
            pltpu.VMEM((n,) + slot, jnp.float32),
            pltpu.SemaphoreType.DMA((local // 64,)), dma, dma, dma, dma,
        ],
        compiler_params=pltpu.CompilerParams(collective_id=0, has_side_effects=True),
    )(band_edges, dm_delays, channel_mask.reshape(1, local), x, ac, as_, bc, bs)
    series = pl.pallas_call(
        series_kernel,
        out_shape=jax.ShapeDtypeStruct((share, steps, LANES), jnp.float32),
        in_specs=[VMEM] * 4,
        out_specs=VMEM,
    )(summed, fc, fs, g)
    return series.reshape(beams, share, samples)


def solution(mesh):
    return jax.shard_map(
        functools.partial(body, mesh.shape["wide"]),
        mesh=mesh,
        in_specs=(P("beam", "wide", None), P(("beam", "wide")), P(), P()),
        out_specs=P("beam", "wide", None),
        check_vma=False,
    )
```
